32 devices in a mesh: grp: 2 (over y), dev: 8 (over z, core), pair: 2 (over x), sub: 1.
Axes of the slice: x: 2, y: 2, z: 4, core: 2. Of those that a mesh axis runs over, the one named last changes fastest.
Arguments:
- queries: bfloat16 [256, 4096], P(('grp', 'dev', 'sub'), 'pair'), parts along dimension 0, may hold values from -6 to 6
- key_rows: bfloat16 [256, 4096], P(('grp', 'dev', 'sub'), 'pair'), parts along dimension 0, may hold values from -6 to 6
- value_rows: bfloat16 [256, 4096], P(('grp', 'dev', 'sub'), 'pair'), parts along dimension 0, may hold values from -6 to 6
- states: float32 [64, 32, 128, 128], P(('grp', 'dev', 'sub'), 'pair'), parts along dimension 0, may hold values from -6 to 6
- decay_rates: float32 [32], P('pair'), may hold values from 0.02 to 2
- head_gain: float32 [4096], P('pair'), may hold values from 0.5 to 1.5
- out_weight: bfloat16 [4096, 6144], P('pair', ('dev', 'sub')), may hold values from -0.09375 to 0.09375
- residual: bfloat16 [256, 6144], P(('grp', 'dev', 'pair', 'sub')), parts along dimension 0, may hold values from -6 to 6
- norm_gain: float32 [6144], replicated, may hold values from 0.5 to 1.5
- expert_ids: int32 [256, 2], P(('grp', 'dev', 'pair', 'sub')), parts along dimension 0, may hold values from 0 to 3, all different within a row; in each aligned block of 8 rows (0 to 7, 8 to 15, ...) at most 4 rows name the same one
- gate_weights: float32 [256, 2], P(('grp', 'dev', 'pair', 'sub')), parts along dimension 0, may hold values from 0.1 to 1
- expert_gate: bfloat16 [18432, 6144], P(('dev', 'pair', 'sub')), may hold values from -0.078125 to 0.078125
- expert_up: bfloat16 [18432, 6144], P(('dev', 'pair', 'sub')), may hold values from -0.078125 to 0.078125
- expert_down: bfloat16 [18432, 6144], P(('dev', 'pair', 'sub')), may hold values from -0.09375 to 0.09375
Outputs:
- layer_out: bfloat16 [256, 6144], P(('grp', 'dev', 'pair', 'sub')), parts along dimension 0
The draws below stay inside these ranges and needn't reach their ends.
There are 2 independent parts, one for each index of `grp`. The reference program is written for one: setup_inputs(seed, part) draws one part's arguments, and reference() takes and returns one part's arrays. A program takes and returns all parts, laid end to end along the dimension named above; an argument that names none is the same for every part. Nothing has to cross between parts.
Inputs may be any that keep to these rules, and one draw needn't show every extreme that they name: `expert_ids`: each row names 2 different experts. In each aligned block of 8 rows (the rows of one device) no expert is named by more than 4 rows, and in every draw some block has an expert named by exactly 4 rows.
All inputs are finite; a program needn't handle non-finite values.
Results may differ from the reference program's by a relative error of at most 0.0048.
Values may be sent and summed in bfloat16 or wider, within the bound.
A program may use at most 128 MiB of HBM per device.

```python
import math
import jax
import jax.numpy as jnp
import numpy as np
from jax import lax

D = 6144
HEADS = 32
HD = 128
FF = 4608
TOPK = 2
EXPERTS = 4
REQUESTS = 32
TOKENS = 128
ROWS = 8
CAP = 4
N_DEV = 8
N_PAIR = 2
N_SUB = 1


def steps_of(stream_key, dims, cuts, least, high):
    loudness, own = 1.0, jax.random.fold_in(stream_key, 6)
    for position, shards_of in cuts:
        steps = jnp.exp(jax.random.uniform(jax.random.fold_in(own, position), (shards_of,), jnp.float32, least / len(cuts), high / len(cuts)))
        loudness = loudness * jnp.repeat(steps, dims[position] // shards_of).reshape([-1 if axis == position else 1 for axis in range(len(dims))])
    return loudness


def routed_block(stream_key, own, number, rows, amount, top, bound, slope):
    order = jax.random.permutation(stream_key, amount)
    packed, common = shares(amount, rows * top, bound, slope, True), shares(amount, rows * top, bound, slope, False)
    places = jnp.arange(amount)

    def named(tallies, offset_by):
        used = int((tallies > 0).sum())
        fixed = max(1, used // 4)
        shifted = fixed + (places - fixed + offset_by * (used - fixed)) % max(1, amount - fixed)
        return jnp.zeros((amount,), jnp.int32).at[order[jnp.where(places < fixed, places, shifted)]].set(jnp.asarray(tallies, jnp.int32))

    tallies = jnp.where(number % 4 == 0, named(packed, number // 4), named(common, number - number // 4 - 1))
    mixed = jax.random.permutation(jax.random.fold_in(own, 3), amount)
    source_of, receiver = mixed[0:amount // 2 * 2:2], mixed[1:amount // 2 * 2:2]
    room = jnp.minimum(tallies[source_of] - 1, bound - tallies[receiver]) // 2
    room = jnp.where((source_of == order[0]) | (receiver == order[0]) | (tallies[receiver] == 0), 0, jnp.maximum(room, 0))
    shifted = jax.random.randint(jax.random.fold_in(own, 4), (amount // 2,), 0, 1 << 20) % (room + 1)
    tallies = tallies.at[source_of].add(-shifted).at[receiver].add(shifted)
    members = jnp.searchsorted(jnp.cumsum(tallies), jnp.arange(rows * top), side="right").astype(jnp.int32)
    table = members.reshape(top, rows).T
    table = table[jax.random.permutation(jax.random.fold_in(own, 1), rows)]
    offset_by = jax.random.randint(jax.random.fold_in(own, 2), (rows, 1), 0, top)
    return jnp.take_along_axis(table, (jnp.arange(top)[None, :] + offset_by) % top, axis=1)


def shares(count, total, bound, lean, full):
    portions = [(1 << 20) // math.isqrt(grade ** lean) + 1 for grade in range(1, count + 1)]
    largest = bound if full else min(bound, max(-(-total // count), total * portions[0] // sum(portions)))
    least = 1 if total - largest >= count - 1 else 0
    holding, surplus = [largest] + [least] * (count - 1), total - largest - least * (count - 1)
    while surplus > 0:
        movable = [i for i in range(1, count) if holding[i] < largest] or [i for i in range(1, count) if holding[i] < bound]
        pool, left = sum([portions[i] for i in movable]), surplus
        for i in movable:
            addition = min(bound - holding[i], max(1, left * portions[i] // pool), surplus)
            holding[i] = holding[i] + addition
            surplus = surplus - addition
    return np.array(holding)


def noise(stream_key, extent, scale, reach, cuts=(), kind=jnp.bfloat16):
    factor_of = steps_of(stream_key, extent, cuts, -0.22, 0.18) if cuts else 1.0
    values = jax.random.normal(stream_key, extent, jnp.float32) * scale * factor_of
    return jnp.minimum(jnp.maximum(values, -reach), reach).astype(kind)


def setup_inputs(seed: int = 0, part: int = 0) -> dict:
    arg_keys = jax.random.split(jax.random.key(seed), 15)
    part_keys = jax.random.split(jax.random.fold_in(arg_keys[14], part), 15)
    queries = noise(part_keys[0], (TOKENS, HEADS * HD), 1.0, 6.0, ((0, 8), (1, 2)))
    key_rows = noise(part_keys[1], (TOKENS, HEADS * HD), 1.0, 6.0, ((0, 8), (1, 2)))
    value_rows = noise(part_keys[2], (TOKENS, HEADS * HD), 1.0, 6.0, ((0, 8), (1, 2)))
    states = noise(part_keys[3], (REQUESTS, HEADS, HD, HD), 1.0, 6.0, ((0, 8), (1, 2)), jnp.float32)
    decay_rates = jnp.clip(jnp.exp(math.log(2.0) - 4.6051702 * jax.random.uniform(arg_keys[4], (HEADS,), jnp.float32) ** steps_of(arg_keys[4], (HEADS,), ((0, 2),), -0.2, 0.2)), 0.02, 2.0)
    head_gain = jnp.clip(1.0 + 0.1 * jax.random.normal(arg_keys[5], (HEADS * HD,), jnp.float32), 0.5, 1.5)
    out_weight = noise(arg_keys[6], (HEADS * HD, D), (HEADS * HD) ** -0.5, 0.09375, ((0, 2), (1, 8)))
    residual = noise(part_keys[7], (TOKENS, D), 1.0, 6.0, ((0, 16),))
    norm_gain = jnp.clip(1.0 + 0.1 * jax.random.normal(arg_keys[8], (D,), jnp.float32), 0.5, 1.5)
    expert_ids_keys = jax.random.split(jax.random.fold_in(part_keys[9], 1), TOKENS // ROWS)
    expert_ids_turns = jax.random.permutation(jax.random.fold_in(part_keys[9], 3), TOKENS // ROWS)
    expert_ids = jax.vmap(lambda own, number: routed_block(jax.random.fold_in(part_keys[9], 2), own, number, ROWS, EXPERTS, TOPK, CAP, 2))(expert_ids_keys, expert_ids_turns).reshape((TOKENS, TOPK))
    gate_weights = jnp.clip(0.1 + 0.9 * jax.random.uniform(part_keys[10], (TOKENS, TOPK), jnp.float32) ** steps_of(part_keys[10], (TOKENS, TOPK), ((0, 16),), -0.2, 0.2), 0.1, 1.0)
    expert_gate = noise(arg_keys[11], (EXPERTS * FF, D), D ** -0.5, 0.078125, ((0, 16),))
    expert_up = noise(arg_keys[12], (EXPERTS * FF, D), D ** -0.5, 0.078125, ((0, 16),))
    expert_down = noise(arg_keys[13], (EXPERTS * FF, D), FF ** -0.5, 0.09375, ((0, 16),))
    return {"queries": queries, "key_rows": key_rows, "value_rows": value_rows, "states": states, "decay_rates": decay_rates, "head_gain": head_gain, "out_weight": out_weight, "residual": residual, "norm_gain": norm_gain, "expert_ids": expert_ids, "gate_weights": gate_weights, "expert_gate": expert_gate, "expert_up": expert_up, "expert_down": expert_down}


EPSILON = 1e-06
HIGHEST = lax.Precision.HIGHEST

def attend(queries, key_rows, value_rows, states, decay_rates, head_gain):
    requests = states.shape[0]
    head_count = states.shape[1]
    head_size = states.shape[2]
    positions = queries.shape[0] // requests
    layout = (requests, positions, head_count, head_size)
    query_plain = queries.reshape(layout)
    key_plain = key_rows.reshape(layout)
    query_float = query_plain.astype(jnp.float32)
    value_float = value_rows.reshape(layout).astype(jnp.float32)
    offsets = jnp.arange(positions, dtype=jnp.float32)
    carried = jnp.exp(-decay_rates[None, :] * (offsets[:, None] + 1.0))
    from_state = jnp.einsum('rphk,rhkv->rphv', query_float, states, precision=HIGHEST)
    from_state = from_state * carried[None, :, :, None]
    scores = jnp.einsum('rthk,rjhk->rhtj', query_plain, key_plain, preferred_element_type=jnp.float32)
    distance = offsets[:, None] - offsets[None, :]
    fading = jnp.exp(-decay_rates[:, None, None] * jnp.maximum(distance, 0.0)[None, :, :])
    fading = jnp.where(distance[None, :, :] >= 0.0, fading, 0.0)
    scores = scores * fading[None]
    within = jnp.einsum('rhtj,rjhv->rthv', scores, value_float, precision=HIGHEST)
    mixed_heads = from_state + within
    spread = lax.optimization_barrier(jnp.mean(mixed_heads * mixed_heads, axis=3, keepdims=True))
    normal = mixed_heads * lax.rsqrt(spread + EPSILON) * head_gain.reshape(head_count, head_size)[None, None]
    return normal.astype(jnp.bfloat16).reshape(requests * positions, head_count * head_size)

def rms_scale(combined, norm_gain):
    spread = lax.optimization_barrier(jnp.mean(combined * combined, axis=-1, keepdims=True))
    return (combined * lax.rsqrt(spread + EPSILON) * norm_gain).astype(jnp.bfloat16)

def expert_apply(picked, gate_part, up_part, down_part):
    leading = picked.shape
    flattened = picked.reshape(-1, leading[-1])
    contract = (((1,), (1,)), ((), ()))
    gate_value = lax.dot_general(flattened, gate_part, contract, preferred_element_type=jnp.float32)
    lifted = lax.dot_general(flattened, up_part, contract, preferred_element_type=jnp.float32)
    hidden = (jax.nn.silu(gate_value) * lifted).astype(jnp.bfloat16)
    output = jnp.dot(hidden, down_part, preferred_element_type=jnp.float32)
    return output.reshape(leading)

def reference(queries, key_rows, value_rows, states, decay_rates, head_gain, out_weight, residual, norm_gain, expert_ids, gate_weights, expert_gate, expert_up, expert_down):
    attended = attend(queries, key_rows, value_rows, states, decay_rates, head_gain)
    projected = jnp.dot(attended, out_weight, preferred_element_type=jnp.float32)
    combined = residual.astype(jnp.float32) + projected
    normed = rms_scale(combined, norm_gain)
    chosen_ids = expert_ids.reshape(-1).astype(jnp.int32)
    repeated = jnp.repeat(normed, TOPK, axis=0)
    most_rows = N_DEV * N_PAIR * N_SUB * CAP
    ladder = jnp.arange(most_rows, dtype=jnp.int32)

    def add_expert(expert, totals):
        expert = jnp.asarray(expert).astype(jnp.int32)
        chosen = (chosen_ids == expert).astype(jnp.int32)
        ranking = (jnp.cumsum(chosen) - 1).astype(jnp.int32)
        placing = ((ranking[None, :] == ladder[:, None]) & (chosen[None, :] == 1)).astype(jnp.bfloat16)
        picked = jnp.dot(placing, repeated, preferred_element_type=jnp.float32).astype(jnp.bfloat16)
        offset = (expert * FF).astype(jnp.int32)
        gate_part = lax.dynamic_slice_in_dim(expert_gate, offset, FF, 0)
        up_part = lax.dynamic_slice_in_dim(expert_up, offset, FF, 0)
        down_part = lax.dynamic_slice_in_dim(expert_down, offset, FF, 0)
        output = expert_apply(picked, gate_part, up_part, down_part)
        back = lax.dot_general(placing.astype(jnp.float32), output, (((0,), (0,)), ((), ())), precision=HIGHEST, preferred_element_type=jnp.float32)
        return totals + back
    totals = lax.fori_loop(0, EXPERTS, add_expert, jnp.zeros((TOKENS * TOPK, D), jnp.float32))
    weighted = totals * gate_weights.reshape(-1)[:, None]
    mixture = lax.optimization_barrier(jnp.sum(weighted.reshape(TOKENS, TOPK, D), axis=1))
    return (combined + mixture).astype(jnp.bfloat16)
```

```python
import functools

import jax
import jax.numpy as jnp
from jax import lax
from jax.experimental import pallas as pl
from jax.experimental.pallas import tpu as pltpu
from jax.sharding import PartitionSpec as P

EPSILON = 1e-06
HIGHEST = lax.Precision.HIGHEST


def attend(queries, key_rows, value_rows, states, decay_rates, head_gain):
    requests = states.shape[0]
    head_count = states.shape[1]
    head_size = states.shape[2]
    positions = queries.shape[0] // requests
    layout = (requests, positions, head_count, head_size)
    query_plain = queries.reshape(layout)
    key_plain = key_rows.reshape(layout)
    query_float = query_plain.astype(jnp.float32)
    value_float = value_rows.reshape(layout).astype(jnp.float32)
    offsets = jnp.arange(positions, dtype=jnp.float32)
    carried = jnp.exp(-decay_rates[None, :] * (offsets[:, None] + 1.0))
    from_state = jnp.einsum("rphk,rhkv->rphv", query_float, states, precision=HIGHEST)
    from_state = from_state * carried[None, :, :, None]
    scores = jnp.einsum(
        "rthk,rjhk->rhtj", query_plain, key_plain, preferred_element_type=jnp.float32
    )
    distance = offsets[:, None] - offsets[None, :]
    fading = jnp.exp(-decay_rates[:, None, None] * jnp.maximum(distance, 0.0)[None, :, :])
    fading = jnp.where(distance[None, :, :] >= 0.0, fading, 0.0)
    scores = scores * fading[None]
    within = jnp.einsum("rhtj,rjhv->rthv", scores, value_float, precision=HIGHEST)
    mixed_heads = from_state + within
    spread = jnp.mean(mixed_heads * mixed_heads, axis=3, keepdims=True)
    normal = (
        mixed_heads
        * lax.rsqrt(spread + EPSILON)
        * head_gain.reshape(head_count, head_size)[None, None]
    )
    return normal.astype(jnp.bfloat16).reshape(requests * positions, head_count * head_size)


def expert_apply(picked, gate_part, up_part, down_part):
    leading = picked.shape
    flattened = picked.reshape(-1, leading[-1])
    contract = (((1,), (1,)), ((), ()))
    gate_value = lax.dot_general(flattened, gate_part, contract, preferred_element_type=jnp.float32)
    lifted = lax.dot_general(flattened, up_part, contract, preferred_element_type=jnp.float32)
    hidden = (jax.nn.silu(gate_value) * lifted).astype(jnp.bfloat16)
    output = jnp.dot(hidden, down_part, preferred_element_type=jnp.float32)
    return output.reshape(leading)


def on_device(
    queries,
    key_rows,
    value_rows,
    states,
    decay_rates,
    head_gain,
    out_weight,
    residual,
    norm_gain,
    expert_ids,
    gate_weights,
    expert_gate,
    expert_up,
    expert_down,
):
    outer_count = lax.axis_size("dev")
    pair_count = lax.axis_size("pair")
    core_count = lax.axis_size("sub")
    attended = attend(queries, key_rows, value_rows, states, decay_rates, head_gain)
    partial_value = jnp.dot(
        lax.all_gather(attended, ("dev", "sub"), axis=0, tiled=True),
        out_weight,
        preferred_element_type=jnp.float32,
    )
    local_rows = residual.shape[0]
    columns = partial_value.shape[1]
    blocks = partial_value.reshape(outer_count, pair_count, core_count, local_rows, columns)
    ordered = jnp.transpose(blocks, (1, 0, 2, 3, 4)).reshape(
        pair_count, outer_count * core_count * local_rows, columns
    )
    shared = lax.psum_scatter(ordered, "pair", scatter_dimension=0, tiled=True)
    shared = shared.reshape(outer_count * core_count, local_rows, columns)
    regrouped = lax.all_to_all(shared, ("dev", "sub"), split_axis=0, concat_axis=2, tiled=True)
    own_rows = regrouped[0]
    combined = residual.astype(jnp.float32) + own_rows
    spread = jnp.mean(combined * combined, axis=-1, keepdims=True)
    normed = (combined * lax.rsqrt(spread + EPSILON) * norm_gain).astype(jnp.bfloat16)
    width = normed.shape[1]
    top_count = expert_ids.shape[1]
    expert_count = outer_count // 2
    capacity = max(2, local_rows * top_count // expert_count)
    chosen_ids = expert_ids.reshape(-1)
    choose = (chosen_ids[:, None] == jnp.arange(expert_count, dtype=jnp.int32)[None, :]).astype(
        jnp.int32
    )
    before = jnp.cumsum(choose, axis=0) - choose
    position = jnp.sum(before * choose, axis=1)
    target = chosen_ids * capacity + position
    placing = (
        target[None, :] == jnp.arange(expert_count * capacity, dtype=jnp.int32)[:, None]
    ).astype(jnp.bfloat16)
    repeated = jnp.repeat(normed, top_count, axis=0)
    packed = jnp.dot(placing, repeated, preferred_element_type=jnp.float32).astype(jnp.bfloat16)
    slot_rows = packed.reshape(expert_count, 1, capacity, width)
    outgoing = jnp.broadcast_to(slot_rows, (expert_count, 2, capacity, width)).reshape(
        outer_count, capacity, width
    )
    partials = expert_apply(
        lax.all_gather(
            lax.all_to_all(outgoing, "dev", split_axis=0, concat_axis=0, tiled=True)[None],
            ("pair", "sub"),
            axis=0,
            tiled=True,
        ),
        expert_gate,
        expert_up,
        expert_down,
    )
    summed_terms = lax.psum_scatter(partials, ("pair", "sub"), scatter_dimension=0, tiled=True)
    returned = lax.all_to_all(summed_terms[0], "dev", split_axis=0, concat_axis=0, tiled=True)
    halves = jnp.sum(returned.reshape(expert_count, -1, capacity, width), axis=1).reshape(
        expert_count * capacity, width
    )
    weighting = placing.astype(jnp.float32) * gate_weights.reshape(-1)[None, :]
    per_slot = lax.dot_general(
        weighting,
        halves,
        (((0,), (0,)), ((), ())),
        precision=HIGHEST,
        preferred_element_type=jnp.float32,
    )
    mixture = jnp.sum(per_slot.reshape(local_rows, top_count, width), axis=1)
    return (combined + mixture).astype(jnp.bfloat16)

MESH = pl.DeviceIdType.MESH
VMEM_BYTES = 67043328
TRANSPOSED = (((1,), (1,)), ((), ()))
LEADING = (((0,), (0,)), ((), ()))


def plan_fits(mesh):
    sizes = mesh.shape
    return sizes["sub"] == 1 and sizes["pair"] == 2 and sizes["dev"] % 2 == 0 and sizes["dev"] > 2


def layer_kernel(
    outer_count,
    queries_hbm,
    keys_hbm,
    values_hbm,
    states_hbm,
    decay_ref,
    head_gain_hbm,
    out_weight_hbm,
    residual_hbm,
    norm_gain_hbm,
    ids_hbm,
    gates_hbm,
    gate_hbm,
    up_hbm,
    down_hbm,
    out_ref,
    queries,
    keys,
    values,
    states,
    head_gain,
    out_weight,
    residual,
    norm_gain,
    ids,
    gates,
    gate,
    up,
    down,
    gathered,
    terms,
    terms_in,
    combined,
    packed,
    routed,
    gate_sum,
    up_sum,
    hidden,
    partial,
    core_out,
    core_in,
    pair_out,
    pair_in,
    owner_out,
    owner_in,
    local_sem,
    gather_send,
    gather_recv,
    terms_send,
    terms_recv,
    route_send,
    route_recv,
    core_send,
    core_recv,
    pair_send,
    pair_recv,
    owner_send,
    owner_recv,
):
    dev = lax.axis_index("dev")
    pair = lax.axis_index("pair")
    plane = dev // 2
    core = dev % 2
    planes = outer_count // 2
    total = outer_count * 2
    me = dev * 2 + pair
    other_core = {"dev": plane * 2 + 1 - core, "pair": pair}
    other_pair = {"dev": dev, "pair": 1 - pair}
    started = []

    def send(source, target, send_sem, recv_sem, where):
        copy = pltpu.make_async_remote_copy(
            src_ref=source,
            dst_ref=target,
            send_sem=send_sem,
            recv_sem=recv_sem,
            device_id=where,
            device_id_type=MESH,
        )
        copy.start()
        started.append(copy)

    def arrived(target, send_sem, recv_sem):
        pltpu.make_async_remote_copy(
            src_ref=target,
            dst_ref=target,
            send_sem=send_sem,
            recv_sem=recv_sem,
            device_id=other_core,
            device_id_type=MESH,
        ).wait_recv()

    loads = [
        pltpu.make_async_copy(source, target, local_sem.at[number])
        for number, (source, target) in enumerate(
            [
                (queries_hbm, queries),
                (keys_hbm, keys),
                (values_hbm, values),
                (states_hbm, states),
                (head_gain_hbm, head_gain),
                (ids_hbm, ids),
                (gates_hbm, gates),
                (residual_hbm, residual),
                (norm_gain_hbm, norm_gain),
                (out_weight_hbm, out_weight),
                (gate_hbm, gate),
                (up_hbm, up),
                (down_hbm, down),
            ]
        )
    ]
    for load in loads:
        load.start()
    barrier = pltpu.get_barrier_semaphore()
    for offset in range(1, total):
        peer = lax.rem(me + offset, total)
        pl.semaphore_signal(
            barrier, inc=1, device_id={"dev": peer // 2, "pair": peer % 2}, device_id_type=MESH
        )
    for load in loads[:5]:
        load.wait()

    requests, heads, size, _ = states.shape
    rows = queries.shape[0]
    positions = rows // requests
    groups = gathered.shape[0]
    group_heads = heads // groups
    row_at = lax.broadcasted_iota(jnp.int32, (rows, rows), 0)
    column_at = lax.broadcasted_iota(jnp.int32, (rows, rows), 1)
    seen = (row_at // positions == column_at // positions) & (column_at <= row_at)
    distance = jnp.maximum(row_at - column_at, 0).astype(jnp.float32)
    wide_row = lax.broadcasted_iota(jnp.int32, (rows, size), 0)
    steps = (wide_row % positions + 1).astype(jnp.float32)

    def one_head(head):
        columns = pl.ds(head * size, size)
        query = queries[:, columns]
        value = values[:, columns]
        rate = decay_ref[head]
        scores = lax.dot_general(
            query, keys[:, columns], TRANSPOSED, preferred_element_type=jnp.float32
        )
        scores = jnp.where(seen, scores * jnp.exp(-rate * distance), 0.0)
        mixed = jnp.zeros((rows, size), jnp.float32)
        query_float = query.astype(jnp.float32)
        for request in range(requests):
            own = jnp.where(wide_row // positions == request, query_float, 0.0)
            mixed = mixed + jnp.dot(
                own.astype(jnp.bfloat16),
                states[request, head].astype(jnp.bfloat16),
                preferred_element_type=jnp.float32,
            )
        mixed = mixed * jnp.exp(-rate * steps) + jnp.dot(
            scores.astype(jnp.bfloat16), value, preferred_element_type=jnp.float32
        )
        spread = jnp.mean(mixed * mixed, axis=1, keepdims=True)
        return (mixed * lax.rsqrt(spread + EPSILON) * head_gain[:, columns]).astype(jnp.bfloat16)

    for group in range(groups):
        for inner in range(group_heads):
            gathered[group, dev, :, inner * size : (inner + 1) * size] = one_head(
                group * group_heads + inner
            )
        if group == 0:
            pl.semaphore_wait(barrier, total - 1)
        mine = gathered.at[group, dev]
        for offset in range(1, planes):
            where = {"dev": lax.rem(plane + offset, planes) * 2 + core, "pair": pair}
            send(mine, mine, gather_send.at[group, offset], gather_recv.at[group, dev], where)
        send(mine, mine, gather_send.at[group, 0], gather_recv.at[group, dev], other_core)

    loads[9].wait()
    width = gathered.shape[3]
    projected = None
    for group in range(groups):
        for offset in range(1, planes):
            source = lax.rem(plane + planes - offset, planes) * 2 + core
            block = gathered.at[group, source]
            arrived(block, gather_send.at[group, 0], gather_recv.at[group, source])
            send(
                block,
                block,
                gather_send.at[group, planes + offset],
                gather_recv.at[group, source],
                other_core,
            )
    for group in range(groups):
        for offset in range(planes):
            source = lax.rem(plane + planes - offset, planes) * 2 + 1 - core
            arrived(
                gathered.at[group, source],
                gather_send.at[group, 0],
                gather_recv.at[group, source],
            )
        product = jnp.dot(
            gathered[group].reshape(outer_count * rows, width),
            out_weight[group * width : (group + 1) * width, :],
            preferred_element_type=jnp.float32,
        )
        projected = product if projected is None else projected + product
    local_rows = residual.shape[0]
    columns = out_weight.shape[1]
    terms[...] = projected.reshape(total, local_rows, columns).astype(jnp.bfloat16)
    for offset in range(1, total):
        owner = lax.rem(me + offset, total)
        send(
            terms.at[owner],
            terms_in.at[me],
            terms_send.at[offset],
            terms_recv.at[me],
            {"dev": owner // 2, "pair": owner % 2},
        )
    terms_in[me] = terms[me]

    for load in loads[5:9]:
        load.wait()
    top_count = ids.shape[1]
    capacity = packed.shape[2]
    slots = planes * capacity
    slot_at = lax.broadcasted_iota(jnp.int32, (local_rows, slots), 1)
    chosen = jnp.zeros((local_rows, slots), jnp.float32)
    weights = jnp.zeros((local_rows, slots), jnp.float32)
    for top in range(top_count):
        named = ids[:, top : top + 1] == slot_at // capacity
        chosen = chosen + jnp.where(named, 1.0, 0.0)
        weights = weights + jnp.where(named, gates[:, top : top + 1], 0.0)
    earlier = jnp.where(
        lax.broadcasted_iota(jnp.int32, (local_rows, local_rows), 1)
        < lax.broadcasted_iota(jnp.int32, (local_rows, local_rows), 0),
        1.0,
        0.0,
    )
    rank = jnp.dot(
        earlier.astype(jnp.bfloat16),
        chosen.astype(jnp.bfloat16),
        preferred_element_type=jnp.float32,
    )
    placed = jnp.abs(rank - (slot_at % capacity).astype(jnp.float32)) < 0.5
    placing = jnp.where(placed, chosen, 0.0)
    weights = jnp.where(placed, weights, 0.0)
    weights_high = weights.astype(jnp.bfloat16)
    weights_low = (weights - weights_high.astype(jnp.float32)).astype(jnp.bfloat16)

    for offset in range(1, total):
        source = lax.rem(me + total - offset, total)
        arrived(terms_in.at[source], terms_send.at[1], terms_recv.at[source])
    squares = jnp.zeros((local_rows, 1), jnp.float32)
    for part in range(outer_count):
        span = slice(part * columns, (part + 1) * columns)
        value = (
            residual[:, span].astype(jnp.float32)
            + terms_in[part * 2].astype(jnp.float32)
            + terms_in[part * 2 + 1].astype(jnp.float32)
        )
        combined[:, span] = value
        squares = squares + jnp.sum(value * value, axis=1, keepdims=True)
    features = combined.shape[1]
    scale = lax.rsqrt(squares / features + EPSILON)

    pieces = packed.shape[0]
    piece = features // pieces
    placing = placing.astype(jnp.bfloat16)

    def slot_of(from_core, from_pair, from_plane):
        return (from_core * 2 + from_pair) * planes + from_plane

    my_slot = slot_of(core, pair, plane)
    for number in range(pieces):
        span = slice(number * piece, (number + 1) * piece)
        normed = (combined[:, span] * scale * norm_gain[:, span]).astype(jnp.bfloat16)
        rows_of = lax.dot_general(placing, normed, LEADING, preferred_element_type=jnp.float32)
        packed[number] = rows_of.reshape(planes, capacity, piece).astype(jnp.bfloat16)
        routed[number, my_slot] = packed[number, plane]
        for offset in range(1, planes):
            expert = lax.rem(plane + offset, planes)
            send(
                packed.at[number, expert],
                routed.at[number, my_slot],
                route_send.at[number, offset],
                route_recv.at[number, my_slot],
                {"dev": expert * 2 + core, "pair": pair},
            )

    def relay_first(number):
        for offset in range(planes):
            slot = slot_of(core, pair, lax.rem(plane + planes - offset, planes))
            block = routed.at[number, slot]
            came = route_recv.at[number, slot]
            if offset:
                arrived(block, route_send.at[number, 0], came)
            send(block, block, route_send.at[number, planes + offset], came, other_pair)
            send(block, block, route_send.at[number, 2 * planes + offset], came, other_core)

    def relay_second(number):
        for offset in range(planes):
            slot = slot_of(core, 1 - pair, lax.rem(plane + planes - offset, planes))
            block = routed.at[number, slot]
            came = route_recv.at[number, slot]
            arrived(block, route_send.at[number, 0], came)
            send(block, block, route_send.at[number, 3 * planes + offset], came, other_core)
        for offset in range(2 * planes):
            slot = slot_of(
                1 - core, offset // planes, lax.rem(plane + planes - offset % planes, planes)
            )
            arrived(routed.at[number, slot], route_send.at[number, 0], route_recv.at[number, slot])

    units = gate.shape[0]
    tile = 128
    slot_rows = total * capacity

    def lift(number):
        span = slice(number * piece, (number + 1) * piece)
        picked = routed[number].reshape(slot_rows, piece)

        def body(step, carry):
            part = pl.ds(pl.multiple_of(step * tile, tile), tile)
            first = lax.dot_general(
                gate[part, span], picked, TRANSPOSED, preferred_element_type=jnp.float32
            )
            second = lax.dot_general(
                up[part, span], picked, TRANSPOSED, preferred_element_type=jnp.float32
            )
            if number:
                first = first + gate_sum[part, :]
                second = second + up_sum[part, :]
            if number < pieces - 1:
                gate_sum[part, :] = first
                up_sum[part, :] = second
            else:
                hidden[part, :] = (first / (1.0 + jnp.exp(-first)) * second).astype(jnp.bfloat16)
            return carry

        lax.fori_loop(0, units // tile, body, 0)

    relay_first(0)
    relay_second(0)
    for number in range(pieces):
        if number + 1 < pieces:
            relay_first(number + 1)
        if number == 0:
            loads[10].wait()
            loads[11].wait()
        lift(number)
        if number + 1 < pieces:
            relay_second(number + 1)
    loads[12].wait()

    chunks = core_out.shape[0]
    chunk = features // chunks
    half = slot_rows // 2
    quarter = half // 2
    kept = core * half
    narrow = chunk // 3 if chunk % 384 == 0 else chunk

    def stage_down(number):
        def body(step, carry):
            part = pl.ds(pl.multiple_of(number * chunk + step * narrow, 128), narrow)
            partial[:, part] = lax.dot_general(
                hidden[...], down[:, part], LEADING, preferred_element_type=jnp.float32
            )
            return carry

        lax.fori_loop(0, chunk // narrow, body, 0)
        span = slice(number * chunk, (number + 1) * chunk)
        core_out[number] = partial[pl.ds(half - kept, half), span].astype(jnp.bfloat16)
        send(
            core_out.at[number],
            core_in.at[number],
            core_send.at[number],
            core_recv.at[number],
            other_core,
        )

    def chip_sum(number, which):
        span = slice(number * chunk, (number + 1) * chunk)
        return partial[pl.ds(kept + which * quarter, quarter), span] + core_in[
            number, pl.ds(which * quarter, quarter), :
        ].astype(jnp.float32)

    def stage_core(number):
        arrived(core_in.at[number], core_send.at[number], core_recv.at[number])
        pair_out[number] = chip_sum(number, 1 - pair).astype(jnp.bfloat16)
        send(
            pair_out.at[number],
            pair_in.at[number],
            pair_send.at[number],
            pair_recv.at[number],
            other_pair,
        )

    def stage_pair(number):
        arrived(pair_in.at[number], pair_send.at[number], pair_recv.at[number])
        value = chip_sum(number, pair) + pair_in[number].astype(jnp.float32)
        owner_out[number] = value.reshape(planes, capacity, chunk).astype(jnp.bfloat16)
        owner_in[number, plane] = owner_out[number, plane]
        for offset in range(1, planes):
            owner = lax.rem(plane + offset, planes)
            send(
                owner_out.at[number, owner],
                owner_in.at[number, plane],
                owner_send.at[number, offset],
                owner_recv.at[number, plane],
                {"dev": owner * 2 + core, "pair": pair},
            )

    def stage_owner(number):
        for offset in range(1, planes):
            expert = lax.rem(plane + planes - offset, planes)
            arrived(
                owner_in.at[number, expert],
                owner_send.at[number, offset],
                owner_recv.at[number, expert],
            )
        span = slice(number * chunk, (number + 1) * chunk)
        result = owner_in[number].reshape(slots, chunk)
        mixture = jnp.dot(weights_high, result, preferred_element_type=jnp.float32) + jnp.dot(
            weights_low, result, preferred_element_type=jnp.float32
        )
        out_ref[:, span] = (combined[:, span] + mixture).astype(jnp.bfloat16)

    for step in range(chunks + 3):
        if step < chunks:
            stage_down(step)
        if 0 <= step - 1 < chunks:
            stage_core(step - 1)
        if 0 <= step - 2 < chunks:
            stage_pair(step - 2)
        if 0 <= step - 3 < chunks:
            stage_owner(step - 3)
    for copy in started:
        copy.wait_send()


def fused_on_device(
    queries,
    key_rows,
    value_rows,
    states,
    decay_rates,
    head_gain,
    out_weight,
    residual,
    norm_gain,
    expert_ids,
    gate_weights,
    expert_gate,
    expert_up,
    expert_down,
):
    outer_count = lax.axis_size("dev")
    planes = outer_count // 2
    total = outer_count * 2
    rows, head_width = queries.shape
    requests, heads, size, _ = states.shape
    local_rows, features = residual.shape
    columns = out_weight.shape[1]
    units = expert_gate.shape[0]
    capacity = max(2, local_rows * expert_ids.shape[1] // planes)
    slot_rows = total * capacity
    groups = 4
    pieces = 2
    chunks = 4
    width = head_width // groups
    piece = features // pieces
    chunk = features // chunks
    half = slot_rows // 2
    low = jnp.bfloat16
    operands = [
        queries,
        key_rows,
        value_rows,
        states,
        decay_rates,
        head_gain.reshape(1, head_width),
        out_weight,
        residual,
        norm_gain.reshape(1, features),
        expert_ids,
        gate_weights,
        expert_gate,
        expert_up,
        expert_down,
    ]
    anywhere = pl.BlockSpec(memory_space=pl.ANY)
    in_specs = [anywhere] * len(operands)
    in_specs[4] = pl.BlockSpec(memory_space=pltpu.SMEM)
    staged = [pltpu.VMEM(x.shape, x.dtype) for i, x in enumerate(operands) if i != 4]
    dma = pltpu.SemaphoreType.DMA
    return pl.pallas_call(
        functools.partial(layer_kernel, outer_count),
        out_shape=jax.ShapeDtypeStruct((local_rows, features), low),
        in_specs=in_specs,
        out_specs=pl.BlockSpec(memory_space=pltpu.VMEM),
        scratch_shapes=staged
        + [
            pltpu.VMEM((groups, outer_count, rows, width), low),
            pltpu.VMEM((total, local_rows, columns), low),
            pltpu.VMEM((total, local_rows, columns), low),
            pltpu.VMEM((local_rows, features), jnp.float32),
            pltpu.VMEM((pieces, planes, capacity, piece), low),
            pltpu.VMEM((pieces, total, capacity, piece), low),
            pltpu.VMEM((units, slot_rows), jnp.float32),
            pltpu.VMEM((units, slot_rows), jnp.float32),
            pltpu.VMEM((units, slot_rows), low),
            pltpu.VMEM((slot_rows, features), jnp.float32),
            pltpu.VMEM((chunks, half, chunk), low),
            pltpu.VMEM((chunks, half, chunk), low),
            pltpu.VMEM((chunks, half // 2, chunk), low),
            pltpu.VMEM((chunks, half // 2, chunk), low),
            pltpu.VMEM((chunks, planes, capacity, chunk), low),
            pltpu.VMEM((chunks, planes, capacity, chunk), low),
            dma((len(operands) - 1,)),
            dma((groups, 2 * planes)),
            dma((groups, outer_count)),
            dma((total,)),
            dma((total,)),
            dma((pieces, 4 * planes)),
            dma((pieces, total)),
            dma((chunks,)),
            dma((chunks,)),
            dma((chunks,)),
            dma((chunks,)),
            dma((chunks, planes)),
            dma((chunks, planes)),
        ],
        compiler_params=pltpu.CompilerParams(
            collective_id=0, has_side_effects=True, vmem_limit_bytes=VMEM_BYTES
        ),
    )(*operands)


def solution(mesh):
    return jax.shard_map(
        fused_on_device if plan_fits(mesh) else on_device,
        mesh=mesh,
        in_specs=(
            P(("grp", "dev", "sub"), "pair"),
            P(("grp", "dev", "sub"), "pair"),
            P(("grp", "dev", "sub"), "pair"),
            P(("grp", "dev", "sub"), "pair", None, None),
            P("pair"),
            P("pair"),
            P("pair", ("dev", "sub")),
            P(("grp", "dev", "pair", "sub"), None),
            P(),
            P(("grp", "dev", "pair", "sub"), None),
            P(("grp", "dev", "pair", "sub"), None),
            P(("dev", "pair", "sub"), None),
            P(("dev", "pair", "sub"), None),
            P(("dev", "pair", "sub"), None),
        ),
        out_specs=P(("grp", "dev", "pair", "sub"), None),
        check_vma=False,
    )
```
